32 devices in a mesh: groups: 2 (over x), seq: 16 (over z, y, core).
Axes of the slice: x: 2, y: 2, z: 4, core: 2. Of those that a mesh axis runs over, the one named last changes fastest.
Arguments:
- atoms: bfloat16 [2, 8192, 128], P('groups', 'seq'), parts along dimension 0, may hold values from -6 to 6
- s_cond: bfloat16 [2048, 768], P(('groups', 'seq')), parts along dimension 0, may hold values from -6 to 6
- token_start: int32 [2048], P(('groups', 'seq')), parts along dimension 0, may hold values from 0 to 8191, as said below
- token_len: int32 [2048], P(('groups', 'seq')), parts along dimension 0, may hold values from 1 to 12, as said below
- atom_mask: int32 [16384], P(('groups', 'seq')), parts along dimension 0, may hold values 0 or 1
- atom_bias: float32 [8, 8192, 128], P('groups', 'seq'), parts along dimension 0, may hold values from -4 to 250
- pair_bias: bfloat16 [32, 1024, 1024], P('groups', 'seq'), parts along dimension 0, may hold values from -4 to 250
- atom_proj: bfloat16 [6, 4, 128, 128], replicated, may hold values from -0.5 to 0.5
- atom_up: bfloat16 [6, 2, 128, 256], replicated, may hold values from -0.5 to 0.5
- atom_down: bfloat16 [6, 256, 128], replicated, may hold values from -0.375 to 0.375
- atom_gains: float32 [6, 2, 128], replicated, may hold values from 0.5 to 1.5
- to_token: bfloat16 [128, 768], replicated, may hold values from -0.5 to 0.5
- token_proj: bfloat16 [4, 768, 768], replicated, may hold values from -0.21875 to 0.21875
- token_gain: float32 [768], replicated, may hold values from 0.5 to 2
- to_atom: bfloat16 [768, 128], replicated, may hold values from -0.21875 to 0.21875
Outputs:
- atoms_out: bfloat16 [2, 8192, 128], P('groups', 'seq'), parts along dimension 0
The draws below stay inside these ranges and needn't reach their ends.
There are 2 independent parts, one for each index of `groups`. The reference program is written for one: setup_inputs(seed, part) draws one part's arguments, and reference() takes and returns one part's arrays. A program takes and returns all parts, laid end to end along the dimension named above; an argument that names none is the same for every part. Nothing has to cross between parts.
Inputs may be any that keep to these rules, and one draw needn't show every extreme that they name: Token t lies in block d = t // 64; its atoms token_start[t] .. token_start[t] + token_len[t] - 1 lie within atoms (d - 1) * 512 .. (d + 2) * 512 - 1 and within the complex. Ranges of the tokens of one block are disjoint and rise with t; ranges of different blocks may share atoms; atoms may belong to no token. `token_len`: every block of 64 tokens has a token of exactly 12 atoms.
All inputs are finite; a program needn't handle non-finite values. No bound on the sum of `atom_mask` on one device may be relied on, other than what follows from the above.
Results may differ from the reference program's by a relative error of at most 0.024.
Values may be sent and summed in bfloat16 or wider, within the bound.
A program may use at most 128 MiB of HBM per device.

```python
import math
import jax
import jax.numpy as jnp
from jax import lax

S = 1
TOK_DEV = 64
MOSTLEN = 12
CA = 128
CT = 768
HT = 16
HA = 4
ATRANS = 256
WQ = 32
WK = 128
ENC_LAYERS = 3
DEC_LAYERS = 3
BLOCKS = 6
AT_DEV = 512
TOKENS = 1024
ATOMS = 8192


def token_ranges(key):
    blocks = TOKENS // TOK_DEV
    lengths = jax.random.randint(jax.random.fold_in(key, 11), (blocks, TOK_DEV), 1, MOSTLEN + 1)
    place = jax.random.randint(jax.random.fold_in(key, 13), (blocks, 1), 0, TOK_DEV)
    lengths = jnp.where(jnp.arange(TOK_DEV)[None, :] == place, MOSTLEN, lengths)
    shifts = jax.random.randint(jax.random.fold_in(key, 12), (blocks,), -(AT_DEV // 2), AT_DEV // 2)
    block_ids = jnp.arange(blocks)
    shifts = jnp.where(block_ids == 0, 0, shifts)
    shifts = jnp.where(block_ids == blocks - 1, -(AT_DEV // 2), shifts)
    inside = jnp.cumsum(lengths, axis=1) - lengths
    starts = block_ids[:, None] * AT_DEV + shifts[:, None] + inside
    return (starts.reshape(-1).astype(jnp.int32), lengths.reshape(-1).astype(jnp.int32))


def biased(key, head_count, row_count, col_count):
    keys_all = jax.random.split(key, 1)
    entries = jnp.clip(jax.random.normal(keys_all[0], (head_count, row_count, col_count), jnp.float32), -4.0, 4.0)
    return entries


def draw_token_start(key, part):
    return token_ranges(key)[0]


def draw_token_len(key, part):
    return token_ranges(key)[1]


def draw_atom_bias(key, part):
    return biased(jax.random.fold_in(key, 21), HA, ATOMS, WK).astype(jnp.float32)


def draw_pair_bias(key, part):
    return biased(jax.random.fold_in(key, 22), HT, TOKENS, TOKENS).astype(jnp.bfloat16)


def touch_ends(values, rng, low, largest):
    spot = [jax.random.randint(jax.random.fold_in(rng, axis), (), 0, length) for axis, length in enumerate(values.shape)]
    main_axis = values.shape.index(max(values.shape))
    beside = spot[:main_axis] + [(spot[main_axis] + 1) % values.shape[main_axis]] + spot[main_axis + 1:]
    return values.at[tuple(spot)].set(low).at[tuple(beside)].set(largest)


def levels(stream_key, dims, shards, least, largest):
    def one(position, parts):
        steps = jax.random.uniform(jax.random.fold_in(jax.random.fold_in(stream_key, 6), position), (parts,), jnp.float32, least / len(shards), largest / len(shards))
        return jnp.repeat(jnp.exp(steps), dims[position] // parts).reshape((-1,) + (1,) * (len(dims) - position - 1))

    loudness = one(*shards[0])
    for cut in shards[1:]:
        loudness = loudness * one(*cut)
    return loudness


def gaussian(stream_key, dims, width, limit, pieces=(), kind=jnp.bfloat16):
    array = width * jax.random.normal(stream_key, dims, jnp.float32)
    if pieces:
        array = array * levels(stream_key, dims, pieces, -0.22, 0.18)
    return jnp.clip(array, -limit, limit).astype(kind)


def setup_inputs(seed: int = 0, part: int = 0) -> dict:
    key_list = jax.random.split(jax.random.key(seed), 16)
    part_keys = jax.random.split(jax.random.fold_in(key_list[15], part), 16)
    atoms = gaussian(part_keys[0], (S, ATOMS, CA), 1.0, 6.0, ((1, 16),))
    s_cond = gaussian(part_keys[1], (TOKENS, CT), 1.0, 6.0, ((0, 16),))
    token_start = draw_token_start(jax.random.fold_in(jax.random.fold_in(key_list[15], part), 71), part)
    token_len = draw_token_len(jax.random.fold_in(jax.random.fold_in(key_list[15], part), 71), part)
    atom_mask = touch_ends((jax.random.randint(part_keys[4], (ATOMS,), 0, 8) < 7).astype(jnp.int32), jax.random.fold_in(part_keys[4], 1), 0, 1)
    atom_bias = draw_atom_bias(jax.random.fold_in(jax.random.fold_in(key_list[15], part), 71), part)
    pair_bias = draw_pair_bias(jax.random.fold_in(jax.random.fold_in(key_list[15], part), 71), part)
    atom_proj = gaussian(key_list[7], (BLOCKS, 4, CA, CA), CA ** -0.5, 0.5)
    atom_up = gaussian(key_list[8], (BLOCKS, 2, CA, ATRANS), CA ** -0.5, 0.5)
    atom_down = gaussian(key_list[9], (BLOCKS, ATRANS, CA), ATRANS ** -0.5, 0.375)
    atom_gains = jnp.clip(1.0 + 0.1 * jax.random.normal(key_list[10], (BLOCKS, 2, CA), jnp.float32), 0.5, 1.5)
    to_token = gaussian(key_list[11], (CA, CT), CA ** -0.5, 0.5)
    token_proj = gaussian(key_list[12], (4, CT, CT), CT ** -0.5, 0.21875)
    token_gain = jnp.clip(jnp.exp(jax.random.uniform(key_list[13], (CT,), jnp.float32, math.log(0.5), math.log(2.0))), 0.5, 2.0)
    to_atom = gaussian(key_list[14], (CT, CA), CT ** -0.5, 0.21875)
    return dict(atoms=atoms, s_cond=s_cond, token_start=token_start, token_len=token_len, atom_mask=atom_mask, atom_bias=atom_bias, pair_bias=pair_bias, atom_proj=atom_proj, atom_up=atom_up, atom_down=atom_down, atom_gains=atom_gains, to_token=to_token, token_proj=token_proj, token_gain=token_gain, to_atom=to_atom)


epsilon = 1e-05
masked = -1000000000.0

def layer_norm(values, gain_vec):
    average = lax.optimization_barrier(jnp.mean(values, axis=-1, keepdims=True))
    centred = values - average
    spread = lax.optimization_barrier(jnp.mean(centred * centred, axis=-1, keepdims=True))
    return centred * lax.rsqrt(spread + epsilon) * gain_vec

def atom_block(stream, key_mask, bias_rows, proj_set, up_pair, down_proj, gain_pair):
    samples, atoms_all, channels = stream.shape
    rim = (WK - WQ) // 2
    head_size = channels // HA
    windows = atoms_all // WQ
    normed = layer_norm(stream, gain_pair[0]).astype(jnp.bfloat16)
    queries = jnp.dot(normed, proj_set[0], preferred_element_type=jnp.float32).astype(jnp.bfloat16)
    key_rows = jnp.dot(normed, proj_set[1], preferred_element_type=jnp.float32).astype(jnp.bfloat16)
    value_rows = jnp.dot(normed, proj_set[2], preferred_element_type=jnp.float32).astype(jnp.bfloat16)
    padded_keys = jnp.pad(key_rows, ((0, 0), (rim, rim), (0, 0)))
    padded_values = jnp.pad(value_rows, ((0, 0), (rim, rim), (0, 0)))
    key_index = (jnp.arange(windows, dtype=jnp.int32) * WQ)[:, None] + jnp.arange(WK, dtype=jnp.int32)[None, :]
    window_mask = jnp.pad(key_mask, (rim, rim))[key_index]
    query_win = queries.reshape(samples, windows, WQ, HA, head_size).astype(jnp.float32)
    keys_win = padded_keys[:, key_index].reshape(samples, windows, WK, HA, head_size).astype(jnp.float32)
    values_win = padded_values[:, key_index].reshape(samples, windows, WK, HA, head_size).astype(jnp.float32)
    scores = jnp.einsum('snqhd,snkhd->snhqk', query_win, keys_win)
    bias_terms = bias_rows.reshape(HA, windows, WQ, WK).transpose(1, 0, 2, 3)[None]
    logits = scores * head_size ** (-0.5) + bias_terms + jnp.where(window_mask == 1, 0.0, masked)[None, :, None, None, :]
    weights = jax.nn.softmax(logits, axis=-1).astype(jnp.bfloat16)
    mixture = jnp.einsum('snhqk,snkhd->snqhd', weights.astype(jnp.float32), values_win)
    mixture = mixture.astype(jnp.bfloat16).reshape(samples, atoms_all, channels)
    stream = stream + jnp.dot(mixture, proj_set[3], preferred_element_type=jnp.float32)
    second = layer_norm(stream, gain_pair[1]).astype(jnp.bfloat16)
    gated = jax.nn.silu(jnp.dot(second, up_pair[0], preferred_element_type=jnp.float32))
    hidden = (gated * jnp.dot(second, up_pair[1], preferred_element_type=jnp.float32)).astype(jnp.bfloat16)
    return stream + jnp.dot(hidden, down_proj, preferred_element_type=jnp.float32)

def block_members(block_id, token_start, token_len):
    window = 3 * AT_DEV
    first_atom = jnp.clip((block_id - 1) * AT_DEV, 0, ATOMS - window).astype(jnp.int32)
    starts = lax.dynamic_slice_in_dim(token_start, (block_id * TOK_DEV).astype(jnp.int32), TOK_DEV)
    lengths = lax.dynamic_slice_in_dim(token_len, (block_id * TOK_DEV).astype(jnp.int32), TOK_DEV)
    positions = first_atom + jnp.arange(window, dtype=jnp.int32)
    member = (positions[None, :] >= starts[:, None]) & (positions[None, :] < (starts + lengths)[:, None])
    return (first_atom, member.astype(jnp.float32), lengths)

def reference(atoms, s_cond, token_start, token_len, atom_mask, atom_bias, pair_bias, atom_proj, atom_up, atom_down, atom_gains, to_token, token_proj, token_gain, to_atom):
    stream = atoms.astype(jnp.float32)
    for block_id in range(ENC_LAYERS):
        stream = atom_block(stream, atom_mask, atom_bias, atom_proj[block_id], atom_up[block_id], atom_down[block_id], atom_gains[block_id])
    encoded = stream.astype(jnp.bfloat16)
    window = 3 * AT_DEV
    block_count = TOKENS // TOK_DEV

    def pool_block(block_id):
        block_id = block_id.astype(jnp.int32)
        first_atom, member, lengths = block_members(block_id, token_start, token_len)
        part_atoms = lax.dynamic_slice_in_dim(encoded, first_atom, window, 1)
        projected = jax.nn.relu(jnp.dot(part_atoms, to_token, preferred_element_type=jnp.float32)).astype(jnp.bfloat16)
        totals = jnp.einsum('ta,sac->stc', member, projected.astype(jnp.float32))
        return totals / lengths[None, :, None].astype(jnp.float32)
    pooled = lax.map(pool_block, jnp.arange(block_count, dtype=jnp.int32))
    features = pooled.transpose(1, 0, 2, 3).reshape(S, TOKENS, CT) + s_cond.astype(jnp.float32)[None]
    normed = layer_norm(features, token_gain).astype(jnp.bfloat16)
    queries = jnp.dot(normed, token_proj[0], preferred_element_type=jnp.float32).astype(jnp.bfloat16)
    key_rows = jnp.dot(normed, token_proj[1], preferred_element_type=jnp.float32).astype(jnp.bfloat16)
    value_rows = jnp.dot(normed, token_proj[2], preferred_element_type=jnp.float32).astype(jnp.bfloat16)
    head_size = CT // HT

    def attend(sample_rows):
        query_one, key_one, value_one = sample_rows
        query_h = query_one.reshape(TOKENS, HT, head_size).astype(jnp.float32).transpose(1, 0, 2)
        key_h = key_one.reshape(TOKENS, HT, head_size).astype(jnp.float32).transpose(1, 0, 2)
        value_h = value_one.reshape(TOKENS, HT, head_size).astype(jnp.float32).transpose(1, 0, 2)

        def one_head(head_rows):
            query_x, key_x, value_x, bias_x = head_rows
            scores = jnp.dot(query_x, key_x.T)
            logits = scores * head_size ** (-0.5) + bias_x.astype(jnp.float32)
            weights = jax.nn.softmax(logits, axis=-1).astype(jnp.bfloat16)
            return jnp.dot(weights.astype(jnp.float32), value_x)
        mixture = lax.map(one_head, (query_h, key_h, value_h, pair_bias))
        return mixture.transpose(1, 0, 2).astype(jnp.bfloat16).reshape(TOKENS, CT)
    token_mix = lax.map(attend, (queries, key_rows, value_rows))
    updated = features + jnp.dot(token_mix, token_proj[3], preferred_element_type=jnp.float32)
    atom_rows = jnp.dot(updated.astype(jnp.bfloat16), to_atom, preferred_element_type=jnp.float32).astype(jnp.bfloat16)

    def spread_block(block_id, running):
        block_id = jnp.asarray(block_id).astype(jnp.int32)
        first_atom, member, lengths = block_members(block_id, token_start, token_len)
        rows_block = lax.dynamic_slice_in_dim(atom_rows, (block_id * TOK_DEV).astype(jnp.int32), TOK_DEV, 1)
        contrib = jnp.einsum('ta,stc->sac', member, rows_block.astype(jnp.float32))
        current = lax.dynamic_slice_in_dim(running, first_atom, window, 1)
        return lax.dynamic_update_slice_in_dim(running, current + contrib, first_atom, 1)
    returned = lax.fori_loop(0, block_count, spread_block, jnp.zeros((S, ATOMS, CA), jnp.float32))
    stream = stream + returned
    for block_id in range(ENC_LAYERS, ENC_LAYERS + DEC_LAYERS):
        stream = atom_block(stream, atom_mask, atom_bias, atom_proj[block_id], atom_up[block_id], atom_down[block_id], atom_gains[block_id])
    return stream.astype(jnp.bfloat16)
```

```python
import functools

import jax
import jax.numpy as jnp
from jax import lax
from jax.experimental import pallas as pl
from jax.experimental.pallas import tpu as pltpu
from jax.sharding import PartitionSpec as P

HT = 16
HA = 4
WQ = 32
WK = 128
ENC_LAYERS = 3
DEC_LAYERS = 3
RIM = (WK - WQ) // 2
GROUP = 4
CHUNK = 256
LANES = 128

epsilon = 1e-05
masked = -1000000000.0
MESH = pl.DeviceIdType.MESH
F32 = jnp.float32
BF16 = jnp.bfloat16


def layer_norm(values, gain_vec):
    average = jnp.mean(values, axis=-1, keepdims=True)
    centred = values - average
    spread = jnp.mean(centred * centred, axis=-1, keepdims=True)
    return centred * lax.rsqrt(spread + epsilon) * gain_vec


def mm(left, right):
    return jnp.dot(left, right, preferred_element_type=F32)


def mm_nt(left, right):
    return lax.dot_general(left, right, (((1,), (1,)), ((), ())), preferred_element_type=F32)


def head_mask(rows, row_size, cols, col_size):
    row_head = lax.broadcasted_iota(jnp.int32, (rows, cols), 0) // row_size
    col_head = lax.broadcasted_iota(jnp.int32, (rows, cols), 1) // col_size
    return row_head == col_head


def kernel(
    count,
    atoms_ref,
    s_cond_ref,
    range_ref,
    mask_ref,
    bias_hbm,
    pair_hbm,
    proj_ref,
    up_ref,
    down_ref,
    gains_ref,
    to_token_ref,
    token_proj_hbm,
    token_gain_ref,
    to_atom_ref,
    out_ref,
    x_ref,
    kv_ref,
    q_ref,
    mix_ref,
    bias_ref,
    pair_ref,
    tp_ref,
    mex_ref,
    wmask_ref,
    rngx_ref,
    encx_ref,
    rowsx_ref,
    uall_ref,
    feat_ref,
    qbd_ref,
    acc_ref,
    max_ref,
    sum_ref,
    load_sem,
    halo_send,
    halo_recv,
    side_send,
    side_recv,
    u_send,
    u_recv,
):
    me = lax.axis_index("seq")
    core = lax.rem(me, 2)
    row_y = lax.rem(me // 2, 2)
    row_z = me // 4
    depth = count // 4
    has_left = me > 0
    has_right = me < count - 1
    atoms_dev = atoms_ref.shape[1]
    channels = atoms_ref.shape[2]
    tokens_dev, width = s_cond_ref.shape
    windows = atoms_dev // WQ
    head_size = channels // HA
    token_head = width // HT
    core_peer = me + 1 - 2 * core
    y_peer = me + 2 - 4 * row_y

    bias_load = pltpu.make_async_copy(bias_hbm, bias_ref, load_sem.at[0])
    tp_load = pltpu.make_async_copy(token_proj_hbm, tp_ref, load_sem.at[1])
    pair_load = pltpu.make_async_copy(pair_hbm, pair_ref, load_sem.at[2])
    bias_load.start()

    barrier = pltpu.get_barrier_semaphore()

    def greet(target):
        pl.semaphore_signal(barrier, inc=1, device_id={"seq": target}, device_id_type=MESH)

    greet(y_peer)
    pl.when(has_left)(lambda: greet(me - 1))
    pl.when(has_right)(lambda: greet(me + 1))
    pl.when(row_z > 0)(lambda: greet(me - 4))
    pl.when(row_z < depth - 1)(lambda: greet(me + 4))
    tp_load.start()
    pair_load.start()

    x_ref[...] = atoms_ref[0].astype(F32)
    mex_ref[1] = mask_ref[...]
    rngx_ref[1] = range_ref[...]

    def clear(slot, edge):
        for ref in (mex_ref, rngx_ref, encx_ref, rowsx_ref):
            ref[slot] = jnp.zeros(ref.shape[1:], ref.dtype)
        for layer in range(ENC_LAYERS + DEC_LAYERS):
            for kind in range(2):
                kv_ref[layer, kind, edge : edge + RIM] = jnp.zeros((RIM, channels), BF16)

    pl.when(jnp.logical_not(has_left))(lambda: clear(0, 0))
    pl.when(jnp.logical_not(has_right))(lambda: clear(2, RIM + atoms_dev))

    peers = 1 + sum(
        jnp.where(there, 1, 0)
        for there in (has_left, has_right, row_z > 0, row_z < depth - 1)
    )
    pl.semaphore_wait(barrier, peers)

    def side_copies(src_left, dst_left, src_right, dst_right, send, recv):
        to_left = pltpu.make_async_remote_copy(
            src_left, dst_left, send(0), recv(0), device_id={"seq": me - 1}, device_id_type=MESH
        )
        to_right = pltpu.make_async_remote_copy(
            src_right, dst_right, send(1), recv(1), device_id={"seq": me + 1}, device_id_type=MESH
        )
        return to_left, to_right

    def start_sides(copies):
        pl.when(has_left)(lambda: copies[0].start())
        pl.when(has_right)(lambda: copies[1].start())

    def receive_sides(copies):
        pl.when(has_right)(lambda: copies[0].wait_recv())
        pl.when(has_left)(lambda: copies[1].wait_recv())

    def sent_sides(copies):
        pl.when(has_left)(lambda: copies[0].wait_send())
        pl.when(has_right)(lambda: copies[1].wait_send())

    def block_sides(src, ref, slot):
        return side_copies(
            src,
            ref.at[2],
            src,
            ref.at[0],
            lambda side: side_send.at[slot, side],
            lambda side: side_recv.at[slot, side],
        )

    def halo_sides(layer):
        return side_copies(
            kv_ref.at[layer, :, pl.ds(RIM, RIM)],
            kv_ref.at[layer, :, pl.ds(RIM + atoms_dev, RIM)],
            kv_ref.at[layer, :, pl.ds(atoms_dev, RIM)],
            kv_ref.at[layer, :, pl.ds(0, RIM)],
            lambda side: halo_send.at[layer, side],
            lambda side: halo_recv.at[layer, side],
        )

    mask_sides = block_sides(mask_ref, mex_ref, 0)
    range_sides = block_sides(range_ref, rngx_ref, 1)
    start_sides(mask_sides)
    start_sides(range_sides)

    def window_masks():
        receive_sides(mask_sides)
        rows = atoms_dev // LANES

        def mask_row(index):
            return mex_ref[index // rows, index % rows : index % rows + 1, :]

        for window in range(windows):
            first = atoms_dev + window * WQ - RIM
            row, offset = first // LANES, first % LANES
            line = mask_row(row)
            if offset:
                line = jnp.concatenate(
                    [line[:, offset:], mask_row(row + 1)[:, :offset]], axis=1
                )
            wmask_ref[window] = jnp.where(line == 1, 0.0, masked).astype(F32)

    atom_heads = head_mask(HA * WQ, WQ, channels, head_size)

    def attend(layer, window):
        first = pl.multiple_of(window * WQ, WQ)
        query = q_ref[pl.ds(first, WQ), :]
        tall = jnp.where(
            atom_heads, jnp.concatenate([query] * HA, axis=0), jnp.zeros((), BF16)
        )
        keys = kv_ref[layer, 0, pl.ds(first, WK), :]
        values = kv_ref[layer, 1, pl.ds(first, WK), :]
        bias = bias_ref[:, pl.ds(first, WQ), :].reshape(HA * WQ, WK)
        logits = mm_nt(tall, keys) * head_size ** (-0.5) + bias + wmask_ref[window]
        weights = jnp.exp(logits - jnp.max(logits, axis=-1, keepdims=True))
        total = jnp.sum(weights, axis=-1, keepdims=True)
        mixed = mm(weights.astype(BF16), values) * (1.0 / total)
        mixed = jnp.where(atom_heads, mixed, 0.0)
        joined = mixed[0:WQ]
        for head in range(1, HA):
            joined = joined + mixed[head * WQ : (head + 1) * WQ]
        mix_ref[pl.ds(first, WQ), :] = joined.astype(BF16)

    def atom_block(layer):
        copies = halo_sides(layer)
        gain = gains_ref[layer]
        for base in range(0, atoms_dev, CHUNK):
            normed = layer_norm(x_ref[base : base + CHUNK], gain[0:1]).astype(BF16)
            for kind in range(2):
                kv_ref[layer, kind, RIM + base : RIM + base + CHUNK] = mm(
                    normed, proj_ref[layer, kind + 1]
                ).astype(BF16)
            q_ref[base : base + CHUNK] = mm(normed, proj_ref[layer, 0]).astype(BF16)
        start_sides(copies)

        def inner(step, carry):
            for part in range(GROUP):
                attend(layer, 2 + step * GROUP + part)
            return carry

        lax.fori_loop(0, (windows - 4) // GROUP, inner, 0)
        receive_sides(copies)
        for window in (0, 1, windows - 2, windows - 1):
            attend(layer, window)
        for base in range(0, atoms_dev, CHUNK):
            stream = x_ref[base : base + CHUNK] + mm(
                mix_ref[base : base + CHUNK], proj_ref[layer, 3]
            )
            second = layer_norm(stream, gain[1:2]).astype(BF16)
            gated = jax.nn.silu(mm(second, up_ref[layer, 0]))
            hidden = (gated * mm(second, up_ref[layer, 1])).astype(BF16)
            x_ref[base : base + CHUNK] = stream + mm(hidden, down_ref[layer])

    def loop_blocks(low, high):
        def step(layer, carry):
            atom_block(layer)
            return carry

        lax.fori_loop(low, high, step, 0)

    window_masks()
    bias_load.wait()
    loop_blocks(0, ENC_LAYERS)

    encx_ref[1] = x_ref[...].astype(BF16)
    enc_sides = block_sides(encx_ref.at[1], encx_ref, 2)
    start_sides(enc_sides)
    receive_sides(range_sides)
    eye = head_mask(tokens_dev, 1, tokens_dev, 1)

    def column(line):
        return jnp.sum(jnp.where(eye, line.astype(F32), 0.0), axis=1, keepdims=True)

    start_col = column(rngx_ref[1, 0:1, 0:tokens_dev])
    end_col = column(rngx_ref[1, 1:2, 0:tokens_dev])

    def pooled(block):
        projected = jnp.maximum(mm(encx_ref[block], to_token_ref[...]), 0.0).astype(BF16)
        place = (me + block - 1) * atoms_dev + lax.broadcasted_iota(
            jnp.int32, (tokens_dev, atoms_dev), 1
        )
        place = place.astype(F32)
        member = jnp.where((place >= start_col) & (place < end_col), 1.0, 0.0).astype(BF16)
        return mm(member, projected)

    totals = pooled(1)
    receive_sides(enc_sides)
    totals = totals + pooled(0) + pooled(2)
    features = totals / (end_col - start_col) + s_cond_ref[...].astype(F32)
    feat_ref[...] = features
    uall_ref[me] = layer_norm(features, token_gain_ref[...]).astype(BF16)

    def at(z, y, c):
        return (z * 2 + y) * 2 + c

    def u_copy(index, target, kind):
        return pltpu.make_async_remote_copy(
            uall_ref.at[index],
            uall_ref.at[index],
            u_send.at[index, kind],
            u_recv.at[index],
            device_id={"seq": target},
            device_id_type=MESH,
        )

    def u_arrived(index):
        u_copy(index, core_peer, 3).wait_recv()

    def own_sends(act):
        pl.when(row_z > 0)(lambda: act(u_copy(me, me - 4, 0)))
        pl.when(row_z < depth - 1)(lambda: act(u_copy(me, me + 4, 1)))
        act(u_copy(me, y_peer, 2))
        act(u_copy(me, core_peer, 3))

    def relay_sends(z, act):
        index = at(z, row_y, core)
        pl.when((z < row_z) & (row_z < depth - 1))(lambda: act(u_copy(index, me + 4, 1)))
        pl.when((z > row_z) & (row_z > 0))(lambda: act(u_copy(index, me - 4, 0)))
        act(u_copy(index, y_peer, 2))
        act(u_copy(index, core_peer, 3))

    def relay(z):
        u_arrived(at(z, row_y, core))
        relay_sends(z, lambda copy: copy.start())

    own_sends(lambda copy: copy.start())

    tp_load.wait()
    half = HT // 2
    half_width = width // 2
    token_heads = head_mask(half * tokens_dev, tokens_dev, half_width, token_head)
    for part in range(2):
        cols = slice(part * half_width, (part + 1) * half_width)
        query = mm(uall_ref[me], tp_ref[0, :, cols]).astype(BF16)
        qbd_ref[part] = jnp.where(
            token_heads, jnp.concatenate([query] * half, axis=0), jnp.zeros((), BF16)
        )
    max_ref[...] = jnp.full_like(max_ref, -1e30)
    sum_ref[...] = jnp.zeros_like(sum_ref)
    acc_ref[...] = jnp.zeros_like(acc_ref)
    pair_load.wait()
    span = 4 * tokens_dev

    def token_block(z):
        rows = uall_ref[pl.ds(4 * z, 4)].reshape(span, width)
        first = pl.multiple_of(z * span, span)
        for part in range(2):
            cols = slice(part * half_width, (part + 1) * half_width)
            keys = mm(rows, tp_ref[1, :, cols]).astype(BF16)
            values = mm(rows, tp_ref[2, :, cols]).astype(BF16)
            bias = pair_ref[part * half : (part + 1) * half, :, pl.ds(first, span)]
            bias = bias.reshape(half * tokens_dev, span).astype(F32)
            logits = mm_nt(qbd_ref[part], keys) * token_head ** (-0.5) + bias
            before = max_ref[part][:, 0:1]
            now = jnp.maximum(before, jnp.max(logits, axis=-1, keepdims=True))
            weights = jnp.exp(logits - now)
            shrink = jnp.exp(before - now)
            total = sum_ref[part][:, 0:1] * shrink + jnp.sum(weights, axis=-1, keepdims=True)
            acc_ref[part] = acc_ref[part] * shrink + mm(weights.astype(BF16), values)
            max_ref[part] = jnp.broadcast_to(now, max_ref.shape[1:])
            sum_ref[part] = jnp.broadcast_to(total, sum_ref.shape[1:])

    def block_done(z):
        across = at(z, 1 - row_y, core)
        u_arrived(across)
        u_copy(across, core_peer, 3).start()
        u_arrived(at(z, row_y, 1 - core))
        u_arrived(at(z, 1 - row_y, 1 - core))
        token_block(z)

    def each_side(distance, act):
        pl.when(row_z - distance >= 0)(lambda: act(row_z - distance))
        pl.when(row_z + distance < depth)(lambda: act(row_z + distance))

    each_side(1, relay)
    block_done(row_z)

    def token_step(distance, carry):
        each_side(distance + 1, relay)
        each_side(distance, block_done)
        return carry

    lax.fori_loop(1, depth, token_step, 0)

    parts = []
    for part in range(2):
        mixed = acc_ref[part] * (1.0 / sum_ref[part][:, 0:1])
        mixed = jnp.where(token_heads, mixed, 0.0)
        joined = mixed[0:tokens_dev]
        for head in range(1, half):
            joined = joined + mixed[head * tokens_dev : (head + 1) * tokens_dev]
        parts.append(joined.astype(BF16))
    token_mix = jnp.concatenate(parts, axis=1)
    updated = feat_ref[...] + mm(token_mix, tp_ref[3])
    rowsx_ref[1] = mm(updated.astype(BF16), to_atom_ref[...]).astype(BF16)
    row_sides = block_sides(rowsx_ref.at[1], rowsx_ref, 3)
    start_sides(row_sides)
    place_own = me * atoms_dev + lax.broadcasted_iota(jnp.int32, (atoms_dev, tokens_dev), 0)
    place_own = place_own.astype(F32)

    def returned(block):
        low = rngx_ref[block, 0:1, 0:tokens_dev].astype(F32)
        high = rngx_ref[block, 1:2, 0:tokens_dev].astype(F32)
        member = jnp.where((place_own >= low) & (place_own < high), 1.0, 0.0).astype(BF16)
        return mm(member, rowsx_ref[block])

    gathered = returned(1)
    receive_sides(row_sides)
    x_ref[...] = x_ref[...] + (gathered + returned(0) + returned(2))

    loop_blocks(ENC_LAYERS, ENC_LAYERS + DEC_LAYERS)
    out_ref[0] = x_ref[...].astype(BF16)

    def sent(copy):
        copy.wait_send()

    for copies in (mask_sides, range_sides, enc_sides, row_sides):
        sent_sides(copies)

    def halo_sent(layer, carry):
        sent_sides(halo_sides(layer))
        return carry

    lax.fori_loop(0, ENC_LAYERS + DEC_LAYERS, halo_sent, 0)
    own_sends(sent)
    sent(u_copy(at(row_z, 1 - row_y, core), core_peer, 3))

    def relay_sent(z):
        relay_sends(z, sent)
        sent(u_copy(at(z, 1 - row_y, core), core_peer, 3))

    def sent_step(distance, carry):
        each_side(distance, relay_sent)
        return carry

    lax.fori_loop(1, depth, sent_step, 0)


def shards(
    count,
    atoms,
    s_cond,
    token_start,
    token_len,
    atom_mask,
    atom_bias,
    pair_bias,
    atom_proj,
    atom_up,
    atom_down,
    atom_gains,
    to_token,
    token_proj,
    token_gain,
    to_atom,
):
    atoms_dev, channels = atoms.shape[1:]
    tokens_dev, width = s_cond.shape
    layers = ENC_LAYERS + DEC_LAYERS
    ranges = jnp.stack([token_start, token_start + token_len])
    ranges = jnp.pad(ranges, ((0, 6), (0, -tokens_dev % LANES)))
    mask_rows = atom_mask.reshape(atoms_dev // LANES, LANES)
    vmem = pl.BlockSpec(memory_space=pltpu.VMEM)
    far = pl.BlockSpec(memory_space=pl.ANY)
    half = HT // 2
    return pl.pallas_call(
        functools.partial(kernel, count),
        out_shape=jax.ShapeDtypeStruct(atoms.shape, BF16),
        in_specs=[vmem, vmem, vmem, vmem, far, far] + [vmem] * 5 + [far, vmem, vmem],
        out_specs=vmem,
        scratch_shapes=[
            pltpu.VMEM((atoms_dev, channels), F32),
            pltpu.VMEM((layers, 2, atoms_dev + 2 * RIM, channels), BF16),
            pltpu.VMEM((atoms_dev, channels), BF16),
            pltpu.VMEM((atoms_dev, channels), BF16),
            pltpu.VMEM(atom_bias.shape, F32),
            pltpu.VMEM(pair_bias.shape, BF16),
            pltpu.VMEM(token_proj.shape, BF16),
            pltpu.VMEM((3,) + mask_rows.shape, jnp.int32),
            pltpu.VMEM((atoms_dev // WQ, 1, WK), F32),
            pltpu.VMEM((3,) + ranges.shape, jnp.int32),
            pltpu.VMEM((3, atoms_dev, channels), BF16),
            pltpu.VMEM((3, tokens_dev, channels), BF16),
            pltpu.VMEM((count, tokens_dev, width), BF16),
            pltpu.VMEM((tokens_dev, width), F32),
            pltpu.VMEM((2, half * tokens_dev, width // 2), BF16),
            pltpu.VMEM((2, half * tokens_dev, width // 2), F32),
            pltpu.VMEM((2, half * tokens_dev, LANES), F32),
            pltpu.VMEM((2, half * tokens_dev, LANES), F32),
            pltpu.SemaphoreType.DMA((3,)),
            pltpu.SemaphoreType.DMA((layers, 2)),
            pltpu.SemaphoreType.DMA((layers, 2)),
            pltpu.SemaphoreType.DMA((4, 2)),
            pltpu.SemaphoreType.DMA((4, 2)),
            pltpu.SemaphoreType.DMA((count, 4)),
            pltpu.SemaphoreType.DMA((count,)),
        ],
        compiler_params=pltpu.CompilerParams(
            collective_id=0, has_side_effects=True, vmem_limit_bytes=60 * 1024 * 1024
        ),
    )(
        atoms,
        s_cond,
        ranges,
        mask_rows,
        atom_bias,
        pair_bias,
        atom_proj,
        atom_up,
        atom_down,
        atom_gains,
        to_token,
        token_proj,
        token_gain.reshape(1, width),
        to_atom,
    )


def solution(mesh):
    placed = (
        P("groups", "seq", None),
        P(("groups", "seq"), None),
        P(("groups", "seq")),
        P(("groups", "seq")),
        P(("groups", "seq")),
        P("groups", "seq", None),
        P("groups", "seq", None),
        P(),
        P(),
        P(),
        P(),
        P(),
        P(),
        P(),
        P(),
    )
    return jax.shard_map(
        functools.partial(shards, mesh.shape["seq"]),
        mesh=mesh,
        in_specs=placed,
        out_specs=P("groups", "seq", None),
        check_vma=False,
    )
```

```python
import functools

import jax
import jax.numpy as jnp
from jax import lax
from jax.experimental import pallas as pl
from jax.experimental.pallas import tpu as pltpu
from jax.sharding import PartitionSpec as P

HT = 16
HA = 4
WQ = 32
WK = 128
ENC_LAYERS = 3
DEC_LAYERS = 3
RIM = (WK - WQ) // 2
GROUP = 4
CHUNK = 256
LANES = 128

epsilon = 1e-05
masked = -1000000000.0
MESH = pl.DeviceIdType.MESH
F32 = jnp.float32
BF16 = jnp.bfloat16


def layer_norm(values, gain_vec):
    average = jnp.mean(values, axis=-1, keepdims=True)
    centred = values - average
    spread = jnp.mean(centred * centred, axis=-1, keepdims=True)
    return centred * lax.rsqrt(spread + epsilon) * gain_vec


def mm(left, right):
    return jnp.dot(left, right, preferred_element_type=F32)


def mm_nt(left, right):
    return lax.dot_general(left, right, (((1,), (1,)), ((), ())), preferred_element_type=F32)


def head_mask(rows, row_size, cols, col_size):
    row_head = lax.broadcasted_iota(jnp.int32, (rows, cols), 0) // row_size
    col_head = lax.broadcasted_iota(jnp.int32, (rows, cols), 1) // col_size
    return row_head == col_head


def kernel(
    count,
    atoms_ref,
    s_cond_ref,
    start_ref,
    length_ref,
    mask_ref,
    bias_hbm,
    pair_hbm,
    proj_ref,
    up_ref,
    down_ref,
    gains_ref,
    to_token_ref,
    token_proj_hbm,
    token_gain_ref,
    to_atom_ref,
    out_ref,
    x_ref,
    kv_ref,
    q_ref,
    mix_ref,
    bias_ref,
    pair_ref,
    tp_ref,
    mex_ref,
    wmask_ref,
    rngx_ref,
    encx_ref,
    rowsx_ref,
    uall_ref,
    feat_ref,
    qbd_ref,
    acc_ref,
    max_ref,
    load_sem,
    halo_send,
    halo_recv,
    side_send,
    side_recv,
    u_send,
    u_recv,
):
    me = lax.axis_index("seq")
    core = lax.rem(me, 2)
    row_y = lax.rem(me // 2, 2)
    row_z = me // 4
    depth = count // 4
    has_left = me > 0
    has_right = me < count - 1
    atoms_dev = atoms_ref.shape[1]
    channels = atoms_ref.shape[2]
    tokens_dev, width = s_cond_ref.shape
    windows = atoms_dev // WQ
    head_size = channels // HA
    token_head = width // HT
    core_peer = me + 1 - 2 * core
    y_peer = me + 2 - 4 * row_y

    bias_load = pltpu.make_async_copy(bias_hbm, bias_ref, load_sem.at[0])
    tp_load = pltpu.make_async_copy(token_proj_hbm, tp_ref, load_sem.at[1])
    pair_load = pltpu.make_async_copy(pair_hbm, pair_ref, load_sem.at[2])
    bias_load.start()

    barrier = pltpu.get_barrier_semaphore()

    def greet(target):
        pl.semaphore_signal(barrier, inc=1, device_id={"seq": target}, device_id_type=MESH)

    greet(y_peer)
    pl.when(has_left)(lambda: greet(me - 1))
    pl.when(has_right)(lambda: greet(me + 1))
    pl.when(row_z > 0)(lambda: greet(me - 4))
    pl.when(row_z < depth - 1)(lambda: greet(me + 4))
    tp_load.start()
    pair_load.start()

    x_ref[...] = atoms_ref[0].astype(F32)
    mex_ref[1] = mask_ref[...].reshape(mex_ref.shape[1:])
    starts = start_ref[...].reshape(1, tokens_dev)
    rngx_ref[1, 0:1, 0:tokens_dev] = starts
    rngx_ref[1, 1:2, 0:tokens_dev] = starts + length_ref[...].reshape(1, tokens_dev)

    def clear(slot, edge):
        for ref in (mex_ref, rngx_ref, encx_ref, rowsx_ref):
            ref[slot] = jnp.zeros(ref.shape[1:], ref.dtype)
        for layer in range(ENC_LAYERS + DEC_LAYERS):
            for kind in range(2):
                kv_ref[layer, kind, edge : edge + RIM] = jnp.zeros((RIM, channels), BF16)

    pl.when(jnp.logical_not(has_left))(lambda: clear(0, 0))
    pl.when(jnp.logical_not(has_right))(lambda: clear(2, RIM + atoms_dev))

    peers = 1 + sum(
        jnp.where(there, 1, 0)
        for there in (has_left, has_right, row_z > 0, row_z < depth - 1)
    )
    pl.semaphore_wait(barrier, peers)

    def side_copies(src_left, dst_left, src_right, dst_right, send, recv):
        to_left = pltpu.make_async_remote_copy(
            src_left, dst_left, send(0), recv(0), device_id={"seq": me - 1}, device_id_type=MESH
        )
        to_right = pltpu.make_async_remote_copy(
            src_right, dst_right, send(1), recv(1), device_id={"seq": me + 1}, device_id_type=MESH
        )
        return to_left, to_right

    def start_sides(copies):
        pl.when(has_left)(lambda: copies[0].start())
        pl.when(has_right)(lambda: copies[1].start())

    def receive_sides(copies):
        pl.when(has_right)(lambda: copies[0].wait_recv())
        pl.when(has_left)(lambda: copies[1].wait_recv())

    def sent_sides(copies):
        pl.when(has_left)(lambda: copies[0].wait_send())
        pl.when(has_right)(lambda: copies[1].wait_send())

    def block_sides(src, ref, slot):
        return side_copies(
            src,
            ref.at[2],
            src,
            ref.at[0],
            lambda side: side_send.at[slot, side],
            lambda side: side_recv.at[slot, side],
        )

    def halo_sides(layer):
        return side_copies(
            kv_ref.at[layer, :, pl.ds(RIM, RIM)],
            kv_ref.at[layer, :, pl.ds(RIM + atoms_dev, RIM)],
            kv_ref.at[layer, :, pl.ds(atoms_dev, RIM)],
            kv_ref.at[layer, :, pl.ds(0, RIM)],
            lambda side: halo_send.at[layer, side],
            lambda side: halo_recv.at[layer, side],
        )

    mask_sides = block_sides(mex_ref.at[1], mex_ref, 0)
    range_sides = block_sides(rngx_ref.at[1], rngx_ref, 1)
    start_sides(mask_sides)
    start_sides(range_sides)

    def window_masks():
        receive_sides(mask_sides)
        rows = atoms_dev // LANES

        def mask_row(index):
            return mex_ref[index // rows, index % rows : index % rows + 1, :]

        for window in range(windows):
            first = atoms_dev + window * WQ - RIM
            row, offset = first // LANES, first % LANES
            line = mask_row(row)
            if offset:
                line = jnp.concatenate(
                    [line[:, offset:], mask_row(row + 1)[:, :offset]], axis=1
                )
            wmask_ref[window] = jnp.where(line == 1, 0.0, masked).astype(F32)

    atom_heads = head_mask(HA * WQ, WQ, channels, head_size)

    def attend(layer, window):
        first = pl.multiple_of(window * WQ, WQ)
        query = q_ref[pl.ds(first, WQ), :]
        tall = jnp.where(
            atom_heads, jnp.concatenate([query] * HA, axis=0), jnp.zeros((), BF16)
        )
        keys = kv_ref[layer, 0, pl.ds(first, WK), :]
        values = jnp.concatenate(
            [kv_ref[layer, 1, pl.ds(first, WK), :], jnp.ones((WK, channels), BF16)], axis=1
        )
        bias = bias_ref[:, pl.ds(first, WQ), :].reshape(HA * WQ, WK)
        logits = mm_nt(tall, keys) * head_size ** (-0.5) + bias + wmask_ref[window]
        weights = jnp.exp(logits - jnp.max(logits, axis=-1, keepdims=True))
        both = mm(weights.astype(BF16), values)
        mixed = jnp.where(atom_heads, both[:, :channels] / both[:, channels:], 0.0)
        joined = mixed[0:WQ]
        for head in range(1, HA):
            joined = joined + mixed[head * WQ : (head + 1) * WQ]
        mix_ref[pl.ds(first, WQ), :] = joined.astype(BF16)

    def atom_block(layer):
        copies = halo_sides(layer)
        gain = gains_ref[layer]
        for base in range(0, atoms_dev, CHUNK):
            normed = layer_norm(x_ref[base : base + CHUNK], gain[0:1]).astype(BF16)
            for kind in range(2):
                kv_ref[layer, kind, RIM + base : RIM + base + CHUNK] = mm(
                    normed, proj_ref[layer, kind + 1]
                ).astype(BF16)
            q_ref[base : base + CHUNK] = mm(normed, proj_ref[layer, 0]).astype(BF16)
        start_sides(copies)

        def inner(step, carry):
            for part in range(GROUP):
                attend(layer, 2 + step * GROUP + part)
            return carry

        lax.fori_loop(0, (windows - 4) // GROUP, inner, 0)
        receive_sides(copies)
        for window in (0, 1, windows - 2, windows - 1):
            attend(layer, window)
        for base in range(0, atoms_dev, CHUNK):
            stream = x_ref[base : base + CHUNK] + mm(
                mix_ref[base : base + CHUNK], proj_ref[layer, 3]
            )
            second = layer_norm(stream, gain[1:2]).astype(BF16)
            gated = jax.nn.silu(mm(second, up_ref[layer, 0]))
            hidden = (gated * mm(second, up_ref[layer, 1])).astype(BF16)
            x_ref[base : base + CHUNK] = stream + mm(hidden, down_ref[layer])

    def loop_blocks(low, high):
        def step(layer, carry):
            atom_block(layer)
            return carry

        lax.fori_loop(low, high, step, 0)

    window_masks()
    bias_load.wait()
    loop_blocks(0, ENC_LAYERS)

    encx_ref[1] = x_ref[...].astype(BF16)
    enc_sides = block_sides(encx_ref.at[1], encx_ref, 2)
    start_sides(enc_sides)
    receive_sides(range_sides)
    eye = head_mask(tokens_dev, 1, tokens_dev, 1)

    def column(line):
        return jnp.sum(jnp.where(eye, line.astype(F32), 0.0), axis=1, keepdims=True)

    start_col = column(rngx_ref[1, 0:1, 0:tokens_dev])
    end_col = column(rngx_ref[1, 1:2, 0:tokens_dev])

    def pooled(block):
        projected = jnp.maximum(mm(encx_ref[block], to_token_ref[...]), 0.0).astype(BF16)
        place = (me + block - 1) * atoms_dev + lax.broadcasted_iota(
            jnp.int32, (tokens_dev, atoms_dev), 1
        )
        place = place.astype(F32)
        member = jnp.where((place >= start_col) & (place < end_col), 1.0, 0.0).astype(BF16)
        return mm(member, projected)

    totals = pooled(1)
    receive_sides(enc_sides)
    totals = totals + pooled(0) + pooled(2)
    features = totals / (end_col - start_col) + s_cond_ref[...].astype(F32)
    feat_ref[...] = features
    uall_ref[me] = layer_norm(features, token_gain_ref[...].reshape(1, width)).astype(BF16)

    def at(z, y, c):
        return (z * 2 + y) * 2 + c

    def u_copy(index, target, kind):
        return pltpu.make_async_remote_copy(
            uall_ref.at[index],
            uall_ref.at[index],
            u_send.at[index, kind],
            u_recv.at[index],
            device_id={"seq": target},
            device_id_type=MESH,
        )

    def u_arrived(index):
        u_copy(index, core_peer, 3).wait_recv()

    def own_sends(act):
        pl.when(row_z > 0)(lambda: act(u_copy(me, me - 4, 0)))
        pl.when(row_z < depth - 1)(lambda: act(u_copy(me, me + 4, 1)))
        act(u_copy(me, y_peer, 2))
        act(u_copy(me, core_peer, 3))

    def relay_sends(z, act):
        index = at(z, row_y, core)
        pl.when((z < row_z) & (row_z < depth - 1))(lambda: act(u_copy(index, me + 4, 1)))
        pl.when((z > row_z) & (row_z > 0))(lambda: act(u_copy(index, me - 4, 0)))
        act(u_copy(index, y_peer, 2))
        act(u_copy(index, core_peer, 3))

    def relay(z):
        u_arrived(at(z, row_y, core))
        relay_sends(z, lambda copy: copy.start())

    own_sends(lambda copy: copy.start())

    tp_load.wait()
    half = HT // 2
    half_width = width // 2
    token_heads = head_mask(half * tokens_dev, tokens_dev, half_width, token_head)
    for part in range(2):
        cols = slice(part * half_width, (part + 1) * half_width)
        query = mm(uall_ref[me], tp_ref[0, :, cols]).astype(BF16)
        qbd_ref[part] = jnp.where(
            token_heads, jnp.concatenate([query] * half, axis=0), jnp.zeros((), BF16)
        )
    max_ref[...] = jnp.full_like(max_ref, -1e30)
    acc_ref[...] = jnp.zeros_like(acc_ref)
    pair_load.wait()
    span = 4 * tokens_dev

    def token_block(z):
        rows = uall_ref[pl.ds(4 * z, 4)].reshape(span, width)
        first = pl.multiple_of(z * span, span)
        for part in range(2):
            cols = slice(part * half_width, (part + 1) * half_width)
            keys = mm(rows, tp_ref[1, :, cols]).astype(BF16)
            values = mm(rows, tp_ref[2, :, cols]).astype(BF16)
            values = jnp.concatenate([values, jnp.ones((span, LANES), BF16)], axis=1)
            bias = pair_ref[part * half : (part + 1) * half, :, pl.ds(first, span)]
            bias = bias.reshape(half * tokens_dev, span).astype(F32)
            logits = mm_nt(qbd_ref[part], keys) * token_head ** (-0.5) + bias
            before = max_ref[part][:, 0:1]
            now = jnp.maximum(before, jnp.max(logits, axis=-1, keepdims=True))
            weights = jnp.exp(logits - now)
            shrink = jnp.exp(before - now)
            acc_ref[part] = acc_ref[part] * shrink + mm(weights.astype(BF16), values)
            max_ref[part] = jnp.broadcast_to(now, max_ref.shape[1:])

    def block_done(z):
        across = at(z, 1 - row_y, core)
        u_arrived(across)
        u_copy(across, core_peer, 3).start()
        u_arrived(at(z, row_y, 1 - core))
        u_arrived(at(z, 1 - row_y, 1 - core))
        token_block(z)

    def each_side(distance, act):
        pl.when(row_z - distance >= 0)(lambda: act(row_z - distance))
        pl.when(row_z + distance < depth)(lambda: act(row_z + distance))

    each_side(1, relay)
    block_done(row_z)

    def token_step(distance, carry):
        each_side(distance + 1, relay)
        each_side(distance, block_done)
        return carry

    lax.fori_loop(1, depth, token_step, 0)

    parts = []
    for part in range(2):
        mixed = acc_ref[part, :, 0:half_width] * (1.0 / acc_ref[part, :, half_width : half_width + 1])
        mixed = jnp.where(token_heads, mixed, 0.0)
        joined = mixed[0:tokens_dev]
        for head in range(1, half):
            joined = joined + mixed[head * tokens_dev : (head + 1) * tokens_dev]
        parts.append(joined.astype(BF16))
    token_mix = jnp.concatenate(parts, axis=1)
    updated = feat_ref[...] + mm(token_mix, tp_ref[3])
    rowsx_ref[1] = mm(updated.astype(BF16), to_atom_ref[...]).astype(BF16)
    row_sides = block_sides(rowsx_ref.at[1], rowsx_ref, 3)
    start_sides(row_sides)
    place_own = me * atoms_dev + lax.broadcasted_iota(jnp.int32, (atoms_dev, tokens_dev), 0)
    place_own = place_own.astype(F32)

    def returned(block):
        low = rngx_ref[block, 0:1, 0:tokens_dev].astype(F32)
        high = rngx_ref[block, 1:2, 0:tokens_dev].astype(F32)
        member = jnp.where((place_own >= low) & (place_own < high), 1.0, 0.0).astype(BF16)
        return mm(member, rowsx_ref[block])

    gathered = returned(1)
    receive_sides(row_sides)
    x_ref[...] = x_ref[...] + (gathered + returned(0) + returned(2))

    loop_blocks(ENC_LAYERS, ENC_LAYERS + DEC_LAYERS)
    out_ref[0] = x_ref[...].astype(BF16)

    def sent(copy):
        copy.wait_send()

    for copies in (mask_sides, range_sides, enc_sides, row_sides):
        sent_sides(copies)

    def halo_sent(layer, carry):
        sent_sides(halo_sides(layer))
        return carry

    lax.fori_loop(0, ENC_LAYERS + DEC_LAYERS, halo_sent, 0)
    own_sends(sent)
    sent(u_copy(at(row_z, 1 - row_y, core), core_peer, 3))

    def relay_sent(z):
        relay_sends(z, sent)
        sent(u_copy(at(z, 1 - row_y, core), core_peer, 3))

    def sent_step(distance, carry):
        each_side(distance, relay_sent)
        return carry

    lax.fori_loop(1, depth, sent_step, 0)


def shards(
    count,
    atoms,
    s_cond,
    token_start,
    token_len,
    atom_mask,
    atom_bias,
    pair_bias,
    atom_proj,
    atom_up,
    atom_down,
    atom_gains,
    to_token,
    token_proj,
    token_gain,
    to_atom,
):
    atoms_dev, channels = atoms.shape[1:]
    tokens_dev, width = s_cond.shape
    layers = ENC_LAYERS + DEC_LAYERS
    vmem = pl.BlockSpec(memory_space=pltpu.VMEM)
    far = pl.BlockSpec(memory_space=pl.ANY)
    half = HT // 2
    return pl.pallas_call(
        functools.partial(kernel, count),
        out_shape=jax.ShapeDtypeStruct(atoms.shape, BF16),
        in_specs=[vmem] * 5 + [far, far] + [vmem] * 5 + [far, vmem, vmem],
        out_specs=vmem,
        scratch_shapes=[
            pltpu.VMEM((atoms_dev, channels), F32),
            pltpu.VMEM((layers, 2, atoms_dev + 2 * RIM, channels), BF16),
            pltpu.VMEM((atoms_dev, channels), BF16),
            pltpu.VMEM((atoms_dev, channels), BF16),
            pltpu.VMEM(atom_bias.shape, F32),
            pltpu.VMEM(pair_bias.shape, BF16),
            pltpu.VMEM(token_proj.shape, BF16),
            pltpu.VMEM((3, atoms_dev // LANES, LANES), jnp.int32),
            pltpu.VMEM((atoms_dev // WQ, 1, WK), F32),
            pltpu.VMEM((3, 8, pl.cdiv(tokens_dev, LANES) * LANES), jnp.int32),
            pltpu.VMEM((3, atoms_dev, channels), BF16),
            pltpu.VMEM((3, tokens_dev, channels), BF16),
            pltpu.VMEM((count, tokens_dev, width), BF16),
            pltpu.VMEM((tokens_dev, width), F32),
            pltpu.VMEM((2, half * tokens_dev, width // 2), BF16),
            pltpu.VMEM((2, half * tokens_dev, width // 2 + LANES), F32),
            pltpu.VMEM((2, half * tokens_dev, LANES), F32),
            pltpu.SemaphoreType.DMA((3,)),
            pltpu.SemaphoreType.DMA((layers, 2)),
            pltpu.SemaphoreType.DMA((layers, 2)),
            pltpu.SemaphoreType.DMA((4, 2)),
            pltpu.SemaphoreType.DMA((4, 2)),
            pltpu.SemaphoreType.DMA((count, 4)),
            pltpu.SemaphoreType.DMA((count,)),
        ],
        compiler_params=pltpu.CompilerParams(
            collective_id=0, has_side_effects=True, vmem_limit_bytes=60 * 1024 * 1024
        ),
    )(
        atoms,
        s_cond,
        token_start,
        token_len,
        atom_mask,
        atom_bias,
        pair_bias,
        atom_proj,
        atom_up,
        atom_down,
        atom_gains,
        to_token,
        token_proj,
        token_gain,
        to_atom,
    )


def solution(mesh):
    placed = (
        P("groups", "seq", None),
        P(("groups", "seq"), None),
        P(("groups", "seq")),
        P(("groups", "seq")),
        P(("groups", "seq")),
        P("groups", "seq", None),
        P("groups", "seq", None),
        P(),
        P(),
        P(),
        P(),
        P(),
        P(),
        P(),
        P(),
    )
    return jax.shard_map(
        functools.partial(shards, mesh.shape["seq"]),
        mesh=mesh,
        in_specs=placed,
        out_specs=P("groups", "seq", None),
        check_vma=False,
    )
```

```python
import functools

import jax
import jax.numpy as jnp
from jax import lax
from jax.experimental import pallas as pl
from jax.experimental.pallas import tpu as pltpu
from jax.sharding import PartitionSpec as P

HT = 16
HA = 4
WQ = 32
WK = 128
ENC_LAYERS = 3
DEC_LAYERS = 3
RIM = (WK - WQ) // 2
CHUNK = 512
LANES = 128

epsilon = 1e-05
masked = -1000000000.0
MESH = pl.DeviceIdType.MESH
F32 = jnp.float32
BF16 = jnp.bfloat16


def layer_norm(values, gain_vec):
    average = jnp.mean(values, axis=-1, keepdims=True)
    centred = values - average
    spread = jnp.mean(centred * centred, axis=-1, keepdims=True)
    return centred * lax.rsqrt(spread + epsilon) * gain_vec


def mm(left, right):
    return jnp.dot(left, right, preferred_element_type=F32)


def mm_nt(left, right):
    return lax.dot_general(left, right, (((1,), (1,)), ((), ())), preferred_element_type=F32)


def head_mask(rows, row_size, cols, col_size):
    row_head = lax.broadcasted_iota(jnp.int32, (rows, cols), 0) // row_size
    col_head = lax.broadcasted_iota(jnp.int32, (rows, cols), 1) // col_size
    return row_head == col_head


def kernel(
    count,
    atoms_ref,
    s_cond_ref,
    start_ref,
    length_ref,
    mask_ref,
    bias_hbm,
    pair_hbm,
    proj_ref,
    up_ref,
    down_ref,
    gains_ref,
    to_token_ref,
    token_proj_hbm,
    token_gain_ref,
    to_atom_ref,
    out_ref,
    x_ref,
    kv_ref,
    q_ref,
    mix_ref,
    bias_ref,
    pair_ref,
    tp_ref,
    mex_ref,
    wmask_ref,
    rngx_ref,
    encx_ref,
    rowsx_ref,
    uall_ref,
    feat_ref,
    qbd_ref,
    acc_ref,
    max_ref,
    load_sem,
    halo_send,
    halo_recv,
    side_send,
    side_recv,
    u_send,
    u_recv,
):
    me = lax.axis_index("seq")
    core = lax.rem(me, 2)
    row_y = lax.rem(me // 2, 2)
    row_z = me // 4
    depth = count // 4
    has_left = me > 0
    has_right = me < count - 1
    atoms_dev = atoms_ref.shape[1]
    channels = atoms_ref.shape[2]
    tokens_dev, width = s_cond_ref.shape
    windows = atoms_dev // WQ
    head_size = channels // HA
    token_head = width // HT
    core_peer = me + 1 - 2 * core
    y_peer = me + 2 - 4 * row_y

    bias_load = pltpu.make_async_copy(bias_hbm, bias_ref, load_sem.at[0])
    tp_load = pltpu.make_async_copy(token_proj_hbm, tp_ref, load_sem.at[1])
    pair_load = pltpu.make_async_copy(pair_hbm, pair_ref, load_sem.at[2])
    bias_load.start()

    barrier = pltpu.get_barrier_semaphore()

    def greet(target):
        pl.semaphore_signal(barrier, inc=1, device_id={"seq": target}, device_id_type=MESH)

    greet(y_peer)
    pl.when(has_left)(lambda: greet(me - 1))
    pl.when(has_right)(lambda: greet(me + 1))
    pl.when(row_z > 0)(lambda: greet(me - 4))
    pl.when(row_z < depth - 1)(lambda: greet(me + 4))
    tp_load.start()
    pair_load.start()

    x_ref[...] = atoms_ref[0].astype(F32)
    mex_ref[1] = mask_ref[...].reshape(mex_ref.shape[1:])
    starts = start_ref[...].reshape(1, tokens_dev)
    rngx_ref[1, 0:1, 0:tokens_dev] = starts
    rngx_ref[1, 1:2, 0:tokens_dev] = starts + length_ref[...].reshape(1, tokens_dev)

    def clear(slot, edge):
        for ref in (mex_ref, rngx_ref, encx_ref, rowsx_ref):
            ref[slot] = jnp.zeros(ref.shape[1:], ref.dtype)
        for layer in range(ENC_LAYERS + DEC_LAYERS):
            for kind in range(2):
                kv_ref[layer, kind, edge : edge + RIM] = jnp.zeros((RIM, channels), BF16)

    pl.when(jnp.logical_not(has_left))(lambda: clear(0, 0))
    pl.when(jnp.logical_not(has_right))(lambda: clear(2, RIM + atoms_dev))

    peers = 1 + sum(
        jnp.where(there, 1, 0)
        for there in (has_left, has_right, row_z > 0, row_z < depth - 1)
    )
    pl.semaphore_wait(barrier, peers)

    def side_copies(src_left, dst_left, src_right, dst_right, send, recv):
        to_left = pltpu.make_async_remote_copy(
            src_left, dst_left, send(0), recv(0), device_id={"seq": me - 1}, device_id_type=MESH
        )
        to_right = pltpu.make_async_remote_copy(
            src_right, dst_right, send(1), recv(1), device_id={"seq": me + 1}, device_id_type=MESH
        )
        return to_left, to_right

    def start_sides(copies):
        pl.when(has_left)(lambda: copies[0].start())
        pl.when(has_right)(lambda: copies[1].start())

    def receive_sides(copies):
        pl.when(has_right)(lambda: copies[0].wait_recv())
        pl.when(has_left)(lambda: copies[1].wait_recv())

    def sent_sides(copies):
        pl.when(has_left)(lambda: copies[0].wait_send())
        pl.when(has_right)(lambda: copies[1].wait_send())

    def block_sides(src, ref, slot):
        return side_copies(
            src,
            ref.at[2],
            src,
            ref.at[0],
            lambda side: side_send.at[slot, side],
            lambda side: side_recv.at[slot, side],
        )

    def halo_sides(layer):
        return side_copies(
            kv_ref.at[layer, :, pl.ds(RIM, RIM)],
            kv_ref.at[layer, :, pl.ds(RIM + atoms_dev, RIM)],
            kv_ref.at[layer, :, pl.ds(atoms_dev, RIM)],
            kv_ref.at[layer, :, pl.ds(0, RIM)],
            lambda side: halo_send.at[layer, side],
            lambda side: halo_recv.at[layer, side],
        )

    mask_sides = block_sides(mex_ref.at[1], mex_ref, 0)
    range_sides = block_sides(rngx_ref.at[1], rngx_ref, 1)
    start_sides(mask_sides)
    start_sides(range_sides)

    def window_masks():
        receive_sides(mask_sides)
        rows = atoms_dev // LANES

        def mask_row(index):
            return mex_ref[index // rows, index % rows : index % rows + 1, :]

        for window in range(windows):
            first = atoms_dev + window * WQ - RIM
            row, offset = first // LANES, first % LANES
            line = mask_row(row)
            if offset:
                line = jnp.concatenate(
                    [line[:, offset:], mask_row(row + 1)[:, :offset]], axis=1
                )
            wmask_ref[window] = jnp.where(line == 1, 0.0, masked).astype(F32)

    atom_heads = head_mask(HA * WQ, WQ, channels, head_size)

    def attend(layer, window):
        first = window * WQ
        query = q_ref[pl.ds(first, WQ), :]
        tall = jnp.where(
            atom_heads, jnp.concatenate([query] * HA, axis=0), jnp.zeros((), BF16)
        )
        keys = kv_ref[layer, 0, pl.ds(first, WK), :]
        values = jnp.concatenate(
            [kv_ref[layer, 1, pl.ds(first, WK), :], jnp.ones((WK, channels), BF16)], axis=1
        )
        bias = bias_ref[:, pl.ds(first, WQ), :].reshape(HA * WQ, WK)
        logits = mm_nt(tall, keys) * head_size ** (-0.5) + bias + wmask_ref[window]
        weights = jnp.exp(logits - jnp.max(logits, axis=-1, keepdims=True))
        both = mm(weights.astype(BF16), values)
        mixed = jnp.where(atom_heads, both[:, :channels] / both[:, channels:], 0.0)
        joined = mixed[0:WQ]
        for head in range(1, HA):
            joined = joined + mixed[head * WQ : (head + 1) * WQ]
        mix_ref[pl.ds(first, WQ), :] = joined.astype(BF16)

    def atom_block(layer):
        copies = halo_sides(layer)
        gain = gains_ref[layer]
        for base in range(0, atoms_dev, CHUNK):
            normed = layer_norm(x_ref[base : base + CHUNK], gain[0:1]).astype(BF16)
            for kind in range(2):
                kv_ref[layer, kind, RIM + base : RIM + base + CHUNK] = mm(
                    normed, proj_ref[layer, kind + 1]
                ).astype(BF16)
            q_ref[base : base + CHUNK] = mm(normed, proj_ref[layer, 0]).astype(BF16)
        start_sides(copies)

        for window in range(2, windows - 2):
            attend(layer, window)
        receive_sides(copies)
        for window in (0, 1, windows - 2, windows - 1):
            attend(layer, window)
        for base in range(0, atoms_dev, CHUNK):
            stream = x_ref[base : base + CHUNK] + mm(
                mix_ref[base : base + CHUNK], proj_ref[layer, 3]
            )
            second = layer_norm(stream, gain[1:2]).astype(BF16)
            gated = jax.nn.silu(mm(second, up_ref[layer, 0]))
            hidden = (gated * mm(second, up_ref[layer, 1])).astype(BF16)
            x_ref[base : base + CHUNK] = stream + mm(hidden, down_ref[layer])

    def loop_blocks(low, high):
        def step(layer, carry):
            atom_block(layer)
            return carry

        lax.fori_loop(low, high, step, 0)

    window_masks()
    bias_load.wait()
    loop_blocks(0, ENC_LAYERS)

    encx_ref[1] = x_ref[...].astype(BF16)
    enc_sides = block_sides(encx_ref.at[1], encx_ref, 2)
    start_sides(enc_sides)
    receive_sides(range_sides)
    eye = head_mask(tokens_dev, 1, tokens_dev, 1)

    def column(line):
        return jnp.sum(jnp.where(eye, line.astype(F32), 0.0), axis=1, keepdims=True)

    start_col = column(rngx_ref[1, 0:1, 0:tokens_dev])
    end_col = column(rngx_ref[1, 1:2, 0:tokens_dev])

    def pooled(block):
        projected = jnp.maximum(mm(encx_ref[block], to_token_ref[...]), 0.0).astype(BF16)
        place = (me + block - 1) * atoms_dev + lax.broadcasted_iota(
            jnp.int32, (tokens_dev, atoms_dev), 1
        )
        place = place.astype(F32)
        member = jnp.where((place >= start_col) & (place < end_col), 1.0, 0.0).astype(BF16)
        return mm(member, projected)

    totals = pooled(1)
    receive_sides(enc_sides)
    totals = totals + pooled(0) + pooled(2)
    features = totals / (end_col - start_col) + s_cond_ref[...].astype(F32)
    feat_ref[...] = features
    uall_ref[me] = layer_norm(features, token_gain_ref[...].reshape(1, width)).astype(BF16)

    def at(z, y, c):
        return (z * 2 + y) * 2 + c

    def u_copy(index, target, kind):
        return pltpu.make_async_remote_copy(
            uall_ref.at[index],
            uall_ref.at[index],
            u_send.at[index, kind],
            u_recv.at[index],
            device_id={"seq": target},
            device_id_type=MESH,
        )

    def u_arrived(index):
        u_copy(index, core_peer, 3).wait_recv()

    def own_sends(act):
        pl.when(row_z > 0)(lambda: act(u_copy(me, me - 4, 0)))
        pl.when(row_z < depth - 1)(lambda: act(u_copy(me, me + 4, 1)))
        act(u_copy(me, y_peer, 2))
        act(u_copy(me, core_peer, 3))

    def relay_sends(z, act):
        index = at(z, row_y, core)
        pl.when((z < row_z) & (row_z < depth - 1))(lambda: act(u_copy(index, me + 4, 1)))
        pl.when((z > row_z) & (row_z > 0))(lambda: act(u_copy(index, me - 4, 0)))
        act(u_copy(index, y_peer, 2))
        act(u_copy(index, core_peer, 3))

    def relay(z):
        u_arrived(at(z, row_y, core))
        relay_sends(z, lambda copy: copy.start())

    own_sends(lambda copy: copy.start())

    tp_load.wait()
    half = HT // 2
    half_width = width // 2
    token_heads = head_mask(half * tokens_dev, tokens_dev, half_width, token_head)
    for part in range(2):
        cols = slice(part * half_width, (part + 1) * half_width)
        query = mm(uall_ref[me], tp_ref[0, :, cols]).astype(BF16)
        qbd_ref[part] = jnp.where(
            token_heads, jnp.concatenate([query] * half, axis=0), jnp.zeros((), BF16)
        )
    max_ref[...] = jnp.full_like(max_ref, -1e30)
    acc_ref[...] = jnp.zeros_like(acc_ref)
    pair_load.wait()
    span = 4 * tokens_dev

    def token_block(z):
        rows = uall_ref[pl.ds(4 * z, 4)].reshape(span, width)
        first = pl.multiple_of(z * span, span)
        for part in range(2):
            cols = slice(part * half_width, (part + 1) * half_width)
            keys = mm(rows, tp_ref[1, :, cols]).astype(BF16)
            values = mm(rows, tp_ref[2, :, cols]).astype(BF16)
            values = jnp.concatenate([values, jnp.ones((span, LANES), BF16)], axis=1)
            bias = pair_ref[part * half : (part + 1) * half, :, pl.ds(first, span)]
            bias = bias.reshape(half * tokens_dev, span).astype(F32)
            logits = mm_nt(qbd_ref[part], keys) * token_head ** (-0.5) + bias
            before = max_ref[part][:, 0:1]
            now = jnp.maximum(before, jnp.max(logits, axis=-1, keepdims=True))
            weights = jnp.exp(logits - now)
            shrink = jnp.exp(before - now)
            acc_ref[part] = acc_ref[part] * shrink + mm(weights.astype(BF16), values)
            max_ref[part] = jnp.broadcast_to(now, max_ref.shape[1:])

    def block_done(z):
        across = at(z, 1 - row_y, core)
        u_arrived(across)
        u_copy(across, core_peer, 3).start()
        u_arrived(at(z, row_y, 1 - core))
        u_arrived(at(z, 1 - row_y, 1 - core))
        token_block(z)

    def each_side(distance, act):
        pl.when(row_z - distance >= 0)(lambda: act(row_z - distance))
        pl.when(row_z + distance < depth)(lambda: act(row_z + distance))

    each_side(1, relay)
    block_done(row_z)

    def token_step(distance, carry):
        each_side(distance + 1, relay)
        each_side(distance, block_done)
        return carry

    lax.fori_loop(1, depth, token_step, 0)

    parts = []
    for part in range(2):
        mixed = acc_ref[part, :, 0:half_width] * (1.0 / acc_ref[part, :, half_width : half_width + 1])
        mixed = jnp.where(token_heads, mixed, 0.0)
        joined = mixed[0:tokens_dev]
        for head in range(1, half):
            joined = joined + mixed[head * tokens_dev : (head + 1) * tokens_dev]
        parts.append(joined.astype(BF16))
    token_mix = jnp.concatenate(parts, axis=1)
    updated = feat_ref[...] + mm(token_mix, tp_ref[3])
    rowsx_ref[1] = mm(updated.astype(BF16), to_atom_ref[...]).astype(BF16)
    row_sides = block_sides(rowsx_ref.at[1], rowsx_ref, 3)
    start_sides(row_sides)
    place_own = me * atoms_dev + lax.broadcasted_iota(jnp.int32, (atoms_dev, tokens_dev), 0)
    place_own = place_own.astype(F32)

    def returned(block):
        low = rngx_ref[block, 0:1, 0:tokens_dev].astype(F32)
        high = rngx_ref[block, 1:2, 0:tokens_dev].astype(F32)
        member = jnp.where((place_own >= low) & (place_own < high), 1.0, 0.0).astype(BF16)
        return mm(member, rowsx_ref[block])

    gathered = returned(1)
    receive_sides(row_sides)
    x_ref[...] = x_ref[...] + (gathered + returned(0) + returned(2))

    loop_blocks(ENC_LAYERS, ENC_LAYERS + DEC_LAYERS)
    out_ref[0] = x_ref[...].astype(BF16)

    def sent(copy):
        copy.wait_send()

    for copies in (mask_sides, range_sides, enc_sides, row_sides):
        sent_sides(copies)

    def halo_sent(layer, carry):
        sent_sides(halo_sides(layer))
        return carry

    lax.fori_loop(0, ENC_LAYERS + DEC_LAYERS, halo_sent, 0)
    own_sends(sent)
    sent(u_copy(at(row_z, 1 - row_y, core), core_peer, 3))

    def relay_sent(z):
        relay_sends(z, sent)
        sent(u_copy(at(z, 1 - row_y, core), core_peer, 3))

    def sent_step(distance, carry):
        each_side(distance, relay_sent)
        return carry

    lax.fori_loop(1, depth, sent_step, 0)


def shards(
    count,
    atoms,
    s_cond,
    token_start,
    token_len,
    atom_mask,
    atom_bias,
    pair_bias,
    atom_proj,
    atom_up,
    atom_down,
    atom_gains,
    to_token,
    token_proj,
    token_gain,
    to_atom,
):
    atoms_dev, channels = atoms.shape[1:]
    tokens_dev, width = s_cond.shape
    layers = ENC_LAYERS + DEC_LAYERS
    vmem = pl.BlockSpec(memory_space=pltpu.VMEM)
    far = pl.BlockSpec(memory_space=pl.ANY)
    half = HT // 2
    return pl.pallas_call(
        functools.partial(kernel, count),
        out_shape=jax.ShapeDtypeStruct(atoms.shape, BF16),
        in_specs=[vmem] * 5 + [far, far] + [vmem] * 5 + [far, vmem, vmem],
        out_specs=vmem,
        scratch_shapes=[
            pltpu.VMEM((atoms_dev, channels), F32),
            pltpu.VMEM((layers, 2, atoms_dev + 2 * RIM, channels), BF16),
            pltpu.VMEM((atoms_dev, channels), BF16),
            pltpu.VMEM((atoms_dev, channels), BF16),
            pltpu.VMEM(atom_bias.shape, F32),
            pltpu.VMEM(pair_bias.shape, BF16),
            pltpu.VMEM(token_proj.shape, BF16),
            pltpu.VMEM((3, atoms_dev // LANES, LANES), jnp.int32),
            pltpu.VMEM((atoms_dev // WQ, 1, WK), F32),
            pltpu.VMEM((3, 8, pl.cdiv(tokens_dev, LANES) * LANES), jnp.int32),
            pltpu.VMEM((3, atoms_dev, channels), BF16),
            pltpu.VMEM((3, tokens_dev, channels), BF16),
            pltpu.VMEM((count, tokens_dev, width), BF16),
            pltpu.VMEM((tokens_dev, width), F32),
            pltpu.VMEM((2, half * tokens_dev, width // 2), BF16),
            pltpu.VMEM((2, half * tokens_dev, width // 2 + LANES), F32),
            pltpu.VMEM((2, half * tokens_dev, LANES), F32),
            pltpu.SemaphoreType.DMA((3,)),
            pltpu.SemaphoreType.DMA((layers, 2)),
            pltpu.SemaphoreType.DMA((layers, 2)),
            pltpu.SemaphoreType.DMA((4, 2)),
            pltpu.SemaphoreType.DMA((4, 2)),
            pltpu.SemaphoreType.DMA((count, 4)),
            pltpu.SemaphoreType.DMA((count,)),
        ],
        compiler_params=pltpu.CompilerParams(
            collective_id=0, has_side_effects=True, vmem_limit_bytes=60 * 1024 * 1024
        ),
    )(
        atoms,
        s_cond,
        token_start,
        token_len,
        atom_mask,
        atom_bias,
        pair_bias,
        atom_proj,
        atom_up,
        atom_down,
        atom_gains,
        to_token,
        token_proj,
        token_gain,
        to_atom,
    )


def solution(mesh):
    placed = (
        P("groups", "seq", None),
        P(("groups", "seq"), None),
        P(("groups", "seq")),
        P(("groups", "seq")),
        P(("groups", "seq")),
        P("groups", "seq", None),
        P("groups", "seq", None),
        P(),
        P(),
        P(),
        P(),
        P(),
        P(),
        P(),
        P(),
    )
    return jax.shard_map(
        functools.partial(shards, mesh.shape["seq"]),
        mesh=mesh,
        in_specs=placed,
        out_specs=P("groups", "seq", None),
        check_vma=False,
    )
```

```python
import functools

import jax
import jax.numpy as jnp
from jax import lax
from jax.experimental import pallas as pl
from jax.experimental.pallas import tpu as pltpu
from jax.sharding import PartitionSpec as P

HT = 16
HA = 4
WQ = 32
WK = 128
ENC_LAYERS = 3
DEC_LAYERS = 3
RIM = (WK - WQ) // 2
LANES = 128

epsilon = 1e-05
masked = -1000000000.0
MESH = pl.DeviceIdType.MESH
F32 = jnp.float32
BF16 = jnp.bfloat16


def layer_norm(values, gain_vec):
    average = jnp.mean(values, axis=-1, keepdims=True)
    centred = values - average
    spread = jnp.mean(centred * centred, axis=-1, keepdims=True)
    return centred * lax.rsqrt(spread + epsilon) * gain_vec


def mm(left, right):
    return jnp.dot(left, right, preferred_element_type=F32)


def mm_nt(left, right):
    return lax.dot_general(left, right, (((1,), (1,)), ((), ())), preferred_element_type=F32)


def head_mask(rows, row_size, cols, col_size):
    row_head = lax.broadcasted_iota(jnp.int32, (rows, cols), 0) // row_size
    col_head = lax.broadcasted_iota(jnp.int32, (rows, cols), 1) // col_size
    return row_head == col_head


def kernel(
    count,
    atoms_ref,
    s_cond_ref,
    start_ref,
    length_ref,
    mask_ref,
    bias_hbm,
    pair_hbm,
    proj_ref,
    up_ref,
    down_ref,
    gains_ref,
    to_token_ref,
    token_proj_hbm,
    token_gain_ref,
    to_atom_ref,
    out_ref,
    x_ref,
    kv_ref,
    q_ref,
    mix_ref,
    bias_ref,
    pair_ref,
    tp_ref,
    mex_ref,
    wmask_ref,
    rngx_ref,
    encx_ref,
    rowsx_ref,
    uall_ref,
    feat_ref,
    qbd_ref,
    acc_ref,
    max_ref,
    load_sem,
    halo_send,
    halo_recv,
    side_send,
    side_recv,
    u_send,
    u_recv,
):
    me = lax.axis_index("seq")
    core = lax.rem(me, 2)
    row_y = lax.rem(me // 2, 2)
    row_z = me // 4
    depth = count // 4
    has_left = me > 0
    has_right = me < count - 1
    atoms_dev = atoms_ref.shape[1]
    channels = atoms_ref.shape[2]
    tokens_dev, width = s_cond_ref.shape
    windows = atoms_dev // WQ
    head_size = channels // HA
    token_head = width // HT
    core_peer = me + 1 - 2 * core
    y_peer = me + 2 - 4 * row_y

    bias_load = pltpu.make_async_copy(bias_hbm, bias_ref, load_sem.at[0])
    tp_load = pltpu.make_async_copy(token_proj_hbm, tp_ref, load_sem.at[1])
    pair_load = pltpu.make_async_copy(pair_hbm, pair_ref, load_sem.at[2])
    bias_load.start()

    barrier = pltpu.get_barrier_semaphore()

    def greet(target):
        pl.semaphore_signal(barrier, inc=1, device_id={"seq": target}, device_id_type=MESH)

    greet(y_peer)
    pl.when(has_left)(lambda: greet(me - 1))
    pl.when(has_right)(lambda: greet(me + 1))
    pl.when(row_z > 0)(lambda: greet(me - 4))
    pl.when(row_z < depth - 1)(lambda: greet(me + 4))
    tp_load.start()
    pair_load.start()

    x_ref[...] = atoms_ref[0].astype(F32)
    mex_ref[1] = mask_ref[...].reshape(mex_ref.shape[1:])
    starts = start_ref[...].reshape(1, tokens_dev)
    rngx_ref[1, 0:1, 0:tokens_dev] = starts
    rngx_ref[1, 1:2, 0:tokens_dev] = starts + length_ref[...].reshape(1, tokens_dev)

    def clear(slot, edge):
        for ref in (mex_ref, rngx_ref, encx_ref, rowsx_ref):
            ref[slot] = jnp.zeros(ref.shape[1:], ref.dtype)
        for layer in range(ENC_LAYERS + DEC_LAYERS):
            for kind in range(2):
                kv_ref[layer, kind, edge : edge + RIM] = jnp.zeros((RIM, channels), BF16)

    pl.when(jnp.logical_not(has_left))(lambda: clear(0, 0))
    pl.when(jnp.logical_not(has_right))(lambda: clear(2, RIM + atoms_dev))

    peers = 1 + sum(
        jnp.where(there, 1, 0)
        for there in (has_left, has_right, row_z > 0, row_z < depth - 1)
    )
    pl.semaphore_wait(barrier, peers)

    def side_copies(src_left, dst_left, src_right, dst_right, send, recv):
        to_left = pltpu.make_async_remote_copy(
            src_left, dst_left, send(0), recv(0), device_id={"seq": me - 1}, device_id_type=MESH
        )
        to_right = pltpu.make_async_remote_copy(
            src_right, dst_right, send(1), recv(1), device_id={"seq": me + 1}, device_id_type=MESH
        )
        return to_left, to_right

    def start_sides(copies):
        pl.when(has_left)(lambda: copies[0].start())
        pl.when(has_right)(lambda: copies[1].start())

    def receive_sides(copies):
        pl.when(has_right)(lambda: copies[0].wait_recv())
        pl.when(has_left)(lambda: copies[1].wait_recv())

    def sent_sides(copies):
        pl.when(has_left)(lambda: copies[0].wait_send())
        pl.when(has_right)(lambda: copies[1].wait_send())

    def block_sides(src, ref, slot):
        return side_copies(
            src,
            ref.at[2],
            src,
            ref.at[0],
            lambda side: side_send.at[slot, side],
            lambda side: side_recv.at[slot, side],
        )

    def halo_sides(layer):
        return side_copies(
            kv_ref.at[layer, :, pl.ds(RIM, RIM)],
            kv_ref.at[layer, :, pl.ds(RIM + atoms_dev, RIM)],
            kv_ref.at[layer, :, pl.ds(atoms_dev, RIM)],
            kv_ref.at[layer, :, pl.ds(0, RIM)],
            lambda side: halo_send.at[layer, side],
            lambda side: halo_recv.at[layer, side],
        )

    mask_sides = block_sides(mex_ref.at[1], mex_ref, 0)
    range_sides = block_sides(rngx_ref.at[1], rngx_ref, 1)
    start_sides(mask_sides)
    start_sides(range_sides)

    def window_masks():
        receive_sides(mask_sides)
        rows = atoms_dev // LANES

        def mask_row(index):
            return mex_ref[index // rows, index % rows : index % rows + 1, :]

        for window in range(windows):
            first = atoms_dev + window * WQ - RIM
            row, offset = first // LANES, first % LANES
            line = mask_row(row)
            if offset:
                line = jnp.concatenate(
                    [line[:, offset:], mask_row(row + 1)[:, :offset]], axis=1
                )
            wmask_ref[window] = jnp.where(line == 1, 0.0, masked).astype(F32)

    atom_heads = head_mask(HA * WQ, WQ, channels, head_size)

    def attend(layer, window):
        first = window * WQ
        query = q_ref[pl.ds(first, WQ), :]
        tall = jnp.where(
            atom_heads, jnp.concatenate([query] * HA, axis=0), jnp.zeros((), BF16)
        )
        keys = kv_ref[layer, 0, pl.ds(first, WK), :]
        values = jnp.concatenate(
            [kv_ref[layer, 1, pl.ds(first, WK), :], jnp.ones((WK, channels), BF16)], axis=1
        )
        bias = bias_ref[:, pl.ds(first, WQ), :].reshape(HA * WQ, WK)
        logits = mm_nt(tall, keys) * head_size ** (-0.5) + bias + wmask_ref[window]
        weights = jnp.exp(logits - jnp.max(logits, axis=-1, keepdims=True))
        both = mm(weights.astype(BF16), values)
        mixed = jnp.where(atom_heads, both[:, :channels] / both[:, channels:], 0.0)
        joined = mixed[0:WQ]
        for head in range(1, HA):
            joined = joined + mixed[head * WQ : (head + 1) * WQ]
        mix_ref[pl.ds(first, WQ), :] = joined.astype(BF16)

    def atom_block(layer):
        copies = halo_sides(layer)
        gain = gains_ref[layer]
        normed = layer_norm(x_ref[...], gain[0:1]).astype(BF16)
        for kind in range(2):
            kv_ref[layer, kind, RIM : RIM + atoms_dev] = mm(
                normed, proj_ref[layer, kind + 1]
            ).astype(BF16)
        start_sides(copies)
        q_ref[...] = mm(normed, proj_ref[layer, 0]).astype(BF16)

        for window in range(2, windows - 2):
            attend(layer, window)
        receive_sides(copies)
        for window in (0, 1, windows - 2, windows - 1):
            attend(layer, window)

        def transition(rows, mixture):
            stream = rows + mm(mixture, proj_ref[layer, 3])
            second = layer_norm(stream, gain[1:2]).astype(BF16)
            gated = jax.nn.silu(mm(second, up_ref[layer, 0]))
            hidden = (gated * mm(second, up_ref[layer, 1])).astype(BF16)
            return stream + mm(hidden, down_ref[layer])

        rim = 2 * WQ
        inside = slice(rim, atoms_dev - rim)
        x_ref[inside] = transition(x_ref[inside], mix_ref[inside])

        def ends(ref):
            return jnp.concatenate([ref[0:rim], ref[atoms_dev - rim : atoms_dev]], axis=0)

        outer = transition(ends(x_ref), ends(mix_ref))
        x_ref[0:rim] = outer[0:rim]
        x_ref[atoms_dev - rim : atoms_dev] = outer[rim:]

    def loop_blocks(low, high):
        def step(layer, carry):
            atom_block(layer)
            return carry

        lax.fori_loop(low, high, step, 0)

    window_masks()
    bias_load.wait()
    loop_blocks(0, ENC_LAYERS)

    encx_ref[1] = x_ref[...].astype(BF16)
    enc_sides = block_sides(encx_ref.at[1], encx_ref, 2)
    start_sides(enc_sides)
    receive_sides(range_sides)
    eye = head_mask(tokens_dev, 1, tokens_dev, 1)

    def column(line):
        return jnp.sum(jnp.where(eye, line.astype(F32), 0.0), axis=1, keepdims=True)

    start_col = column(rngx_ref[1, 0:1, 0:tokens_dev])
    end_col = column(rngx_ref[1, 1:2, 0:tokens_dev])

    def pooled(block):
        projected = jnp.maximum(mm(encx_ref[block], to_token_ref[...]), 0.0).astype(BF16)
        place = (me + block - 1) * atoms_dev + lax.broadcasted_iota(
            jnp.int32, (tokens_dev, atoms_dev), 1
        )
        place = place.astype(F32)
        member = jnp.where((place >= start_col) & (place < end_col), 1.0, 0.0).astype(BF16)
        return mm(member, projected)

    totals = pooled(1)
    receive_sides(enc_sides)
    totals = totals + pooled(0) + pooled(2)
    features = totals / (end_col - start_col) + s_cond_ref[...].astype(F32)
    feat_ref[...] = features
    uall_ref[me] = layer_norm(features, token_gain_ref[...].reshape(1, width)).astype(BF16)

    def at(z, y, c):
        return (z * 2 + y) * 2 + c

    def u_copy(index, target, kind):
        return pltpu.make_async_remote_copy(
            uall_ref.at[index],
            uall_ref.at[index],
            u_send.at[index, kind],
            u_recv.at[index],
            device_id={"seq": target},
            device_id_type=MESH,
        )

    def u_arrived(index):
        u_copy(index, core_peer, 3).wait_recv()

    def own_sends(act):
        pl.when(row_z > 0)(lambda: act(u_copy(me, me - 4, 0)))
        pl.when(row_z < depth - 1)(lambda: act(u_copy(me, me + 4, 1)))
        act(u_copy(me, y_peer, 2))
        act(u_copy(me, core_peer, 3))

    def relay_sends(z, act):
        index = at(z, row_y, core)
        pl.when((z < row_z) & (row_z < depth - 1))(lambda: act(u_copy(index, me + 4, 1)))
        pl.when((z > row_z) & (row_z > 0))(lambda: act(u_copy(index, me - 4, 0)))
        act(u_copy(index, y_peer, 2))
        act(u_copy(index, core_peer, 3))

    def relay(z):
        u_arrived(at(z, row_y, core))
        relay_sends(z, lambda copy: copy.start())

    own_sends(lambda copy: copy.start())

    tp_load.wait()
    half = HT // 2
    half_width = width // 2
    token_heads = head_mask(half * tokens_dev, tokens_dev, half_width, token_head)
    for part in range(2):
        cols = slice(part * half_width, (part + 1) * half_width)
        query = mm(uall_ref[me], tp_ref[0, :, cols]).astype(BF16)
        qbd_ref[part] = jnp.where(
            token_heads, jnp.concatenate([query] * half, axis=0), jnp.zeros((), BF16)
        )
    max_ref[...] = jnp.full_like(max_ref, -1e30)
    acc_ref[...] = jnp.zeros_like(acc_ref)
    pair_load.wait()
    span = 4 * tokens_dev

    def token_block(z):
        rows = uall_ref[pl.ds(4 * z, 4)].reshape(span, width)
        first = pl.multiple_of(z * span, span)
        for part in range(2):
            cols = slice(part * half_width, (part + 1) * half_width)
            keys = mm(rows, tp_ref[1, :, cols]).astype(BF16)
            values = mm(rows, tp_ref[2, :, cols]).astype(BF16)
            values = jnp.concatenate([values, jnp.ones((span, LANES), BF16)], axis=1)
            bias = pair_ref[part * half : (part + 1) * half, :, pl.ds(first, span)]
            bias = bias.reshape(half * tokens_dev, span).astype(F32)
            logits = mm_nt(qbd_ref[part], keys) * token_head ** (-0.5) + bias
            before = max_ref[part][:, 0:1]
            now = jnp.maximum(before, jnp.max(logits, axis=-1, keepdims=True))
            weights = jnp.exp(logits - now)
            shrink = jnp.exp(before - now)
            acc_ref[part] = acc_ref[part] * shrink + mm(weights.astype(BF16), values)
            max_ref[part] = jnp.broadcast_to(now, max_ref.shape[1:])

    def block_done(z):
        across = at(z, 1 - row_y, core)
        u_arrived(across)
        u_copy(across, core_peer, 3).start()
        u_arrived(at(z, row_y, 1 - core))
        u_arrived(at(z, 1 - row_y, 1 - core))
        token_block(z)

    def each_side(distance, act):
        pl.when(row_z - distance >= 0)(lambda: act(row_z - distance))
        pl.when(row_z + distance < depth)(lambda: act(row_z + distance))

    each_side(1, relay)
    block_done(row_z)

    def token_step(distance, carry):
        each_side(distance + 1, relay)
        each_side(distance, block_done)
        return carry

    lax.fori_loop(1, depth, token_step, 0)

    parts = []
    for part in range(2):
        mixed = acc_ref[part, :, 0:half_width] * (1.0 / acc_ref[part, :, half_width : half_width + 1])
        mixed = jnp.where(token_heads, mixed, 0.0)
        joined = mixed[0:tokens_dev]
        for head in range(1, half):
            joined = joined + mixed[head * tokens_dev : (head + 1) * tokens_dev]
        parts.append(joined.astype(BF16))
    token_mix = jnp.concatenate(parts, axis=1)
    updated = feat_ref[...] + mm(token_mix, tp_ref[3])
    rowsx_ref[1] = mm(updated.astype(BF16), to_atom_ref[...]).astype(BF16)
    row_sides = block_sides(rowsx_ref.at[1], rowsx_ref, 3)
    start_sides(row_sides)
    place_own = me * atoms_dev + lax.broadcasted_iota(jnp.int32, (atoms_dev, tokens_dev), 0)
    place_own = place_own.astype(F32)

    def returned(block):
        low = rngx_ref[block, 0:1, 0:tokens_dev].astype(F32)
        high = rngx_ref[block, 1:2, 0:tokens_dev].astype(F32)
        member = jnp.where((place_own >= low) & (place_own < high), 1.0, 0.0).astype(BF16)
        return mm(member, rowsx_ref[block])

    gathered = returned(1)
    receive_sides(row_sides)
    x_ref[...] = x_ref[...] + (gathered + returned(0) + returned(2))

    loop_blocks(ENC_LAYERS, ENC_LAYERS + DEC_LAYERS)
    out_ref[0] = x_ref[...].astype(BF16)

    def sent(copy):
        copy.wait_send()

    for copies in (mask_sides, range_sides, enc_sides, row_sides):
        sent_sides(copies)

    def halo_sent(layer, carry):
        sent_sides(halo_sides(layer))
        return carry

    lax.fori_loop(0, ENC_LAYERS + DEC_LAYERS, halo_sent, 0)
    own_sends(sent)
    sent(u_copy(at(row_z, 1 - row_y, core), core_peer, 3))

    def relay_sent(z):
        relay_sends(z, sent)
        sent(u_copy(at(z, 1 - row_y, core), core_peer, 3))

    def sent_step(distance, carry):
        each_side(distance, relay_sent)
        return carry

    lax.fori_loop(1, depth, sent_step, 0)


def shards(
    count,
    atoms,
    s_cond,
    token_start,
    token_len,
    atom_mask,
    atom_bias,
    pair_bias,
    atom_proj,
    atom_up,
    atom_down,
    atom_gains,
    to_token,
    token_proj,
    token_gain,
    to_atom,
):
    atoms_dev, channels = atoms.shape[1:]
    tokens_dev, width = s_cond.shape
    layers = ENC_LAYERS + DEC_LAYERS
    vmem = pl.BlockSpec(memory_space=pltpu.VMEM)
    far = pl.BlockSpec(memory_space=pl.ANY)
    half = HT // 2
    return pl.pallas_call(
        functools.partial(kernel, count),
        out_shape=jax.ShapeDtypeStruct(atoms.shape, BF16),
        in_specs=[vmem] * 5 + [far, far] + [vmem] * 5 + [far, vmem, vmem],
        out_specs=vmem,
        scratch_shapes=[
            pltpu.VMEM((atoms_dev, channels), F32),
            pltpu.VMEM((layers, 2, atoms_dev + 2 * RIM, channels), BF16),
            pltpu.VMEM((atoms_dev, channels), BF16),
            pltpu.VMEM((atoms_dev, channels), BF16),
            pltpu.VMEM(atom_bias.shape, F32),
            pltpu.VMEM(pair_bias.shape, BF16),
            pltpu.VMEM(token_proj.shape, BF16),
            pltpu.VMEM((3, atoms_dev // LANES, LANES), jnp.int32),
            pltpu.VMEM((atoms_dev // WQ, 1, WK), F32),
            pltpu.VMEM((3, 8, pl.cdiv(tokens_dev, LANES) * LANES), jnp.int32),
            pltpu.VMEM((3, atoms_dev, channels), BF16),
            pltpu.VMEM((3, tokens_dev, channels), BF16),
            pltpu.VMEM((count, tokens_dev, width), BF16),
            pltpu.VMEM((tokens_dev, width), F32),
            pltpu.VMEM((2, half * tokens_dev, width // 2), BF16),
            pltpu.VMEM((2, half * tokens_dev, width // 2 + LANES), F32),
            pltpu.VMEM((2, half * tokens_dev, LANES), F32),
            pltpu.SemaphoreType.DMA((3,)),
            pltpu.SemaphoreType.DMA((layers, 2)),
            pltpu.SemaphoreType.DMA((layers, 2)),
            pltpu.SemaphoreType.DMA((4, 2)),
            pltpu.SemaphoreType.DMA((4, 2)),
            pltpu.SemaphoreType.DMA((count, 4)),
            pltpu.SemaphoreType.DMA((count,)),
        ],
        compiler_params=pltpu.CompilerParams(
            collective_id=0, has_side_effects=True, vmem_limit_bytes=60 * 1024 * 1024
        ),
    )(
        atoms,
        s_cond,
        token_start,
        token_len,
        atom_mask,
        atom_bias,
        pair_bias,
        atom_proj,
        atom_up,
        atom_down,
        atom_gains,
        to_token,
        token_proj,
        token_gain,
        to_atom,
    )


def solution(mesh):
    placed = (
        P("groups", "seq", None),
        P(("groups", "seq"), None),
        P(("groups", "seq")),
        P(("groups", "seq")),
        P(("groups", "seq")),
        P("groups", "seq", None),
        P("groups", "seq", None),
        P(),
        P(),
        P(),
        P(),
        P(),
        P(),
        P(),
        P(),
    )
    return jax.shard_map(
        functools.partial(shards, mesh.shape["seq"]),
        mesh=mesh,
        in_specs=placed,
        out_specs=P("groups", "seq", None),
        check_vma=False,
    )
```
